32 devices in a mesh: seq: 8 (over y, x, core), batch: 4 (over z).
Axes of the slice: x: 2, y: 2, z: 4, core: 2. Of those that a mesh axis runs over, the one named last changes fastest.
Arguments:
- tokens: bfloat16 [16, 1024, 1152], P('batch', 'seq'), may hold values from -6 to 6
- condition: bfloat16 [16, 1152], P('batch'), may hold values from -6 to 6
- segment_ids: int32 [16, 1024], P('batch'), may hold values from 0 to 3, never falling along the last dimension, each value on 1 to 512 neighbouring positions
- cotangent: bfloat16 [16, 1024, 1152], P('batch', 'seq'), may hold values from -6 to 6
- block_slots: int32 [432], replicated, may hold values from 0 to 447, as said below
- modulator_slots: int32 [216], replicated, may hold values from 0 to 223, as said below
- block_low: bfloat16 [448, 32, 1152], P(('seq', 'batch')), may hold values from -0.1875 to 0.1875
- block_master: float32 [448, 32, 1152], P(('seq', 'batch')), may hold values from -0.1875 to 0.1875
- block_first: float32 [448, 32, 1152], P(('seq', 'batch')), may hold values from -0.015625 to 0.015625
- block_second: float32 [448, 32, 1152], P(('seq', 'batch')), may hold values from 5e-07 to 8e-06
- block_ema: float32 [448, 32, 1152], P(('seq', 'batch')), may hold values from -0.1875 to 0.1875
- modulator_low: bfloat16 [224, 32, 1152], P(('seq', 'batch')), may hold values from -0.1875 to 0.1875
- modulator_master: float32 [224, 32, 1152], P(('seq', 'batch')), may hold values from -0.1875 to 0.1875
- modulator_first: float32 [224, 32, 1152], P(('seq', 'batch')), may hold values from -0.015625 to 0.015625
- modulator_second: float32 [224, 32, 1152], P(('seq', 'batch')), may hold values from 5e-07 to 8e-06
- modulator_ema: float32 [224, 32, 1152], P(('seq', 'batch')), may hold values from -0.1875 to 0.1875
- biases: float32 [16128], replicated, may hold values from -4 to 4
- bias_first: float32 [16128], replicated, may hold values from -0.015625 to 0.015625
- bias_second: float32 [16128], replicated, may hold values from 5e-07 to 8e-06
- bias_ema: float32 [16128], replicated, may hold values from -4 to 4
Outputs:
- output: bfloat16 [16, 1024, 1152], P('batch', 'seq')
- tokens_grad: float32 [16, 1024, 1152], P('batch', 'seq')
- condition_grad: float32 [16, 1152], P('batch')
- block_grad: float32 [448, 32, 1152], P(('seq', 'batch'))
- block_new: float32 [448, 32, 1152], P(('seq', 'batch'))
- block_first_new: float32 [448, 32, 1152], P(('seq', 'batch'))
- block_second_new: float32 [448, 32, 1152], P(('seq', 'batch'))
- block_ema_new: float32 [448, 32, 1152], P(('seq', 'batch'))
- block_low_new: bfloat16 [448, 32, 1152], P(('seq', 'batch'))
- modulator_grad: float32 [224, 32, 1152], P(('seq', 'batch'))
- modulator_new: float32 [224, 32, 1152], P(('seq', 'batch'))
- modulator_first_new: float32 [224, 32, 1152], P(('seq', 'batch'))
- modulator_second_new: float32 [224, 32, 1152], P(('seq', 'batch'))
- modulator_ema_new: float32 [224, 32, 1152], P(('seq', 'batch'))
- modulator_low_new: bfloat16 [224, 32, 1152], P(('seq', 'batch'))
- bias_grad: float32 [16128], replicated
- biases_new: float32 [16128], replicated
- bias_first_new: float32 [16128], replicated
- bias_second_new: float32 [16128], replicated
- bias_ema_new: float32 [16128], replicated
The draws below stay inside these ranges and needn't reach their ends.
Inputs may be any that keep to these rules, and one draw needn't show every extreme that they name: Distinct values; tile t lies in slot block_slots[t], held by device slot // 14 of seq+batch. Distinct values; tile t lies in slot modulator_slots[t], held by device slot // 7 of seq+batch. `segment_ids`: never falls along a sequence's tokens.
All inputs are finite; a program needn't handle non-finite values.
Results may differ from the reference program's by a relative error of at most 0.015.
The reference program's roundings to bfloat16 on the way count: a program that leaves them out, or rounds other values in their place, can miss the bound.
Values may be sent and summed in bfloat16 or wider, within the bound.
No kernel may reach another device: no remote copies, remote signals or barrier semaphores. Data moves between devices by JAX's collectives and lax.ppermute only.
A program may use at most 384 MiB of HBM per device.

```python
import math
import jax
import jax.numpy as jnp
import numpy as np
from jax import lax

D = 1152
HEADS = 16
HD = 72
FF = 4608
F = 16
TR = 32
STEP = 5
P_SIZE = 64
L = 1024
SEQS = 16
NT_W = 432
NT_A = 216
SLOT_ALL_W = 448
SLOT_ALL_A = 224
NBIAS = 16128


def spread_slots(key, live_count, slot_total):
    inside_slots = jax.random.permutation(key, slot_total - 2)[:live_count - 2] + 1
    chosen = jnp.concatenate([inside_slots.astype(jnp.int32), jnp.array([0, slot_total - 1], jnp.int32)])
    return jax.random.permutation(jax.random.fold_in(key, 7), chosen).astype(jnp.int32)


def draw_block_slots(key, part):
    return spread_slots(jax.random.fold_in(key, 1), NT_W, SLOT_ALL_W)


def draw_modulator_slots(key, part):
    return spread_slots(jax.random.fold_in(key, 2), NT_A, SLOT_ALL_A)


def block_levels(rng, shape, shards, smallest, top_value):
    def one(axis_at, blocks):
        steps = jax.random.uniform(jax.random.fold_in(jax.random.fold_in(rng, 6), axis_at), (blocks,), jnp.float32, smallest / len(shards), top_value / len(shards))
        return jnp.repeat(jnp.exp(steps), shape[axis_at] // blocks).reshape((-1,) + (1,) * (len(shape) - axis_at - 1))

    loudness = one(*shards[0])
    for cut in shards[1:]:
        loudness = loudness * one(*cut)
    return loudness


def split_up(amount, total, reach, skew):
    loads = [(1 << 20) // math.isqrt(rank ** skew) + 1 for rank in range(2, amount + 1)]
    surplus, given = total - reach - (amount - 1), [1] * (amount - 1)
    while surplus > 0:
        free = [i for i in range(amount - 1) if given[i] < reach]
        mass, left = sum([loads[i] for i in free]), surplus
        for i in free:
            more = min(reach - given[i], max(1, left * loads[i] // mass), surplus)
            given[i] = given[i] + more
            surplus = surplus - more
    return np.array([reach] + given)


def ragged_sizes(rng, number_of, total, reach, skew):
    if number_of == 2:
        one = jax.random.randint(rng, (), max(1, total - reach), min(reach, total - 1) + 1)
        return jnp.stack([one, total - one])
    tallies = jnp.asarray(split_up(number_of, total, reach, skew), jnp.int32)
    couples = (number_of - 1) // 2
    donor, receiver = tallies[1:1 + 2 * couples:2], tallies[2:2 + 2 * couples:2]
    slack = jnp.minimum(donor - 1, reach - receiver)
    shifted = jax.random.randint(jax.random.fold_in(rng, 1), (couples,), 0, 1 << 20) % (slack + 1)
    tallies = tallies.at[1:1 + 2 * couples:2].set(donor - shifted).at[2:2 + 2 * couples:2].set(receiver + shifted)
    return tallies[jax.random.permutation(jax.random.fold_in(rng, 2), number_of)]


def noise(own_key, shape, scale, limit, cuts=(), held_as=jnp.bfloat16):
    level = block_levels(own_key, shape, cuts, -0.22, 0.18) if cuts else 1.0
    values = jax.random.normal(own_key, shape, jnp.float32) * scale * level
    return jnp.minimum(jnp.maximum(values, -limit), limit).astype(held_as)


def setup_inputs(seed: int = 0) -> dict:
    arg_keys = jax.random.split(jax.random.key(seed), 21)
    tokens = noise(arg_keys[0], (SEQS, L, D), 1.0, 6.0, ((0, 4), (1, 8)))
    condition = noise(arg_keys[1], (SEQS, D), 1.0, 6.0, ((0, 4),))
    segment_ids = jax.vmap(lambda own: jnp.searchsorted(jnp.cumsum(ragged_sizes(own, max(3, F // 4), L, L // 2, 0)), jnp.arange(L), side="right"))(jax.random.split(arg_keys[2], SEQS)).reshape((SEQS, L)).astype(jnp.int32)
    cotangent = noise(arg_keys[3], (SEQS, L, D), 1.0, 6.0, ((0, 4), (1, 8)))
    block_slots = draw_block_slots(jax.random.fold_in(arg_keys[20], 71), 0)
    modulator_slots = draw_modulator_slots(jax.random.fold_in(arg_keys[20], 71), 0)
    block_low = noise(arg_keys[6], (SLOT_ALL_W, TR, D), D ** -0.5, 0.1875, ((0, 32),))
    block_master = noise(arg_keys[7], (SLOT_ALL_W, TR, D), D ** -0.5, 0.1875, ((0, 32),), jnp.float32)
    block_first = noise(arg_keys[8], (SLOT_ALL_W, TR, D), 0.001, 0.015625, ((0, 32),), jnp.float32)
    block_second = jnp.clip(jnp.exp(math.log(7.999999979801942e-06) - 2.7725887 * jax.random.uniform(arg_keys[9], (SLOT_ALL_W, TR, D), jnp.float32) ** block_levels(arg_keys[9], (SLOT_ALL_W, TR, D), ((0, 32),), -0.2, 0.2)), 4.999999987376214e-07, 7.999999979801942e-06)
    block_ema = noise(arg_keys[10], (SLOT_ALL_W, TR, D), D ** -0.5, 0.1875, ((0, 32),), jnp.float32)
    modulator_low = noise(arg_keys[11], (SLOT_ALL_A, TR, D), D ** -0.5, 0.1875, ((0, 32),))
    modulator_master = noise(arg_keys[12], (SLOT_ALL_A, TR, D), D ** -0.5, 0.1875, ((0, 32),), jnp.float32)
    modulator_first = noise(arg_keys[13], (SLOT_ALL_A, TR, D), 0.001, 0.015625, ((0, 32),), jnp.float32)
    modulator_second = jnp.clip(jnp.exp(math.log(7.999999979801942e-06) - 2.7725887 * jax.random.uniform(arg_keys[14], (SLOT_ALL_A, TR, D), jnp.float32) ** block_levels(arg_keys[14], (SLOT_ALL_A, TR, D), ((0, 32),), -0.2, 0.2)), 4.999999987376214e-07, 7.999999979801942e-06)
    modulator_ema = noise(arg_keys[15], (SLOT_ALL_A, TR, D), D ** -0.5, 0.1875, ((0, 32),), jnp.float32)
    biases = noise(arg_keys[16], (NBIAS,), 0.3, 4.0, (), jnp.float32)
    bias_first = noise(arg_keys[17], (NBIAS,), 0.001, 0.015625, (), jnp.float32)
    bias_second = jnp.clip(jnp.exp(jax.random.uniform(arg_keys[18], (NBIAS,), jnp.float32, math.log(4.999999987376214e-07), math.log(7.999999979801942e-06))), 4.999999987376214e-07, 7.999999979801942e-06)
    bias_ema = noise(arg_keys[19], (NBIAS,), 0.3, 4.0, (), jnp.float32)
    return dict(tokens=tokens, condition=condition, segment_ids=segment_ids, cotangent=cotangent, block_slots=block_slots, modulator_slots=modulator_slots, block_low=block_low, block_master=block_master, block_first=block_first, block_second=block_second, block_ema=block_ema, modulator_low=modulator_low, modulator_master=modulator_master, modulator_first=modulator_first, modulator_second=modulator_second, modulator_ema=modulator_ema, biases=biases, bias_first=bias_first, bias_second=bias_second, bias_ema=bias_ema)


ln_eps = 1e-06
adam_eps = 1e-08
beta_one = 0.5
beta_two = 0.5
learn_rate = 0.01
bias_rate = 0.1
decay_rate = 0.1
ema_rate = 0.9
clip_rms = 0.001
highest = lax.Precision.HIGHEST

@jax.custom_vjp
def low(v):
    return lax.optimization_barrier(v.astype(jnp.bfloat16)).astype(jnp.float32)

@jax.custom_vjp
def low_back(v):
    return v

def low_keep(v):
    return (low(v), None)

def low_pass(kept, grad):
    return (grad,)

def back_keep(v):
    return (v, None)

def back_low(kept, grad):
    return (low(grad),)
low.defvjp(low_keep, low_pass)
low_back.defvjp(back_keep, back_low)

def swish(values):
    return values * jax.nn.sigmoid(values)

def norm_rows(values):
    center = values - lax.optimization_barrier(jnp.mean(values, axis=-1, keepdims=True))
    return center * lax.rsqrt(lax.optimization_barrier(jnp.mean(center * center, axis=-1, keepdims=True)) + ln_eps)

def sequence_forward(seq_tokens, cond_vec, w_qkv, w_out, w_up, w_down, w_mod, bias_vec, same_seg):
    cond_act = low(swish(cond_vec))
    modul = jnp.dot(cond_act, w_mod.T, precision=highest) + bias_vec[:6 * D]
    shift_one, scale_one, gate_one, shift_two, scale_two, gate_two = jnp.split(modul, 6)
    act_one = low(low_back(norm_rows(seq_tokens) * (1.0 + scale_one) + shift_one))
    qkv_bias = jnp.concatenate([bias_vec[6 * D:7 * D], jnp.zeros((D,), jnp.float32), bias_vec[7 * D:8 * D]])
    qkv = jnp.dot(act_one, w_qkv.T, precision=highest) + qkv_bias
    query = low(low_back(qkv[:, :D])).reshape(F, -1, HEADS, HD)
    keyed = low(low_back(qkv[:, D:2 * D])).reshape(F, -1, HEADS, HD)
    valued = low(low_back(qkv[:, 2 * D:])).reshape(F, -1, HEADS, HD)
    scores = low_back(jnp.einsum('fphd,gphd->phfg', query, keyed, precision=highest) * HD ** (-0.5))
    masked = jnp.where(same_seg[:, None], scores, -1e+30)
    top_score = lax.optimization_barrier(jnp.max(masked, axis=-1, keepdims=True))
    exps = jnp.exp(masked - top_score)
    probs = low(exps / lax.optimization_barrier(jnp.sum(exps, axis=-1, keepdims=True)))
    attended = jnp.einsum('phfg,gphd->fphd', probs, valued, precision=highest).reshape(-1, D)
    attended = low(low_back(attended))
    attention_out = low(low_back(jnp.dot(attended, w_out.T, precision=highest) + bias_vec[8 * D:9 * D]))
    middle = seq_tokens + gate_one * attention_out
    act_two = low(norm_rows(middle) * (1.0 + scale_two) + shift_two)
    pre_up = low_back(jnp.dot(act_two, w_up.T, precision=highest) + bias_vec[9 * D:9 * D + FF])
    gelu_low = low(jax.nn.gelu(pre_up, approximate=True))
    down = low_back(jnp.dot(gelu_low, w_down, precision=highest) + bias_vec[9 * D + FF:])
    return middle + gate_two * down

def clip_factor(square_sum, count):
    return jnp.minimum(1.0, clip_rms * lax.rsqrt(square_sum / count + 1e-12))

def adam_rule(grads, clip, master, first, second, ema_old, live, rate):
    used = grads * clip
    first_new = beta_one * first + (1.0 - beta_one) * used
    second_new = beta_two * second + (1.0 - beta_two) * used * used
    fix_one = 1.0 - beta_one ** STEP
    fix_two = 1.0 - beta_two ** STEP
    step_size = rate * (first_new / fix_one / (jnp.sqrt(second_new / fix_two) + adam_eps) + decay_rate * master)
    master_new = master - step_size
    ema_new = ema_rate * ema_old + (1.0 - ema_rate) * master_new
    return (grads * live, master_new * live, first_new * live, second_new * live, ema_new * live, (master_new * live).astype(jnp.bfloat16))

def reference(tokens, condition, segment_ids, cotangent, block_slots, modulator_slots, block_low, block_master, block_first, block_second, block_ema, modulator_low, modulator_master, modulator_first, modulator_second, modulator_ema, biases, bias_first, bias_second, bias_ema):
    block_rows = block_low.astype(jnp.float32)[block_slots].reshape(NT_W * TR, D)
    w_qkv = block_rows[:3 * D]
    w_out = block_rows[3 * D:4 * D]
    w_up = block_rows[4 * D:4 * D + FF]
    w_down = block_rows[4 * D + FF:]
    w_mod = modulator_low.astype(jnp.float32)[modulator_slots].reshape(6 * D, D)
    params = (w_qkv, w_out, w_up, w_down, w_mod, biases)

    def one_sequence(carry, item):
        seq_tokens, cond_vec, seq_ids, seq_cot = item
        ids_grid = seq_ids.reshape(F, P_SIZE).T
        same_seg = ids_grid[:, :, None] == ids_grid[:, None, :]

        def forward(tok_f, cond_f, wq, wo, wu, wd, wm, bias_vec):
            return sequence_forward(tok_f, cond_f, wq, wo, wu, wd, wm, bias_vec, same_seg)
        result, pullback = jax.vjp(forward, seq_tokens.astype(jnp.float32), cond_vec.astype(jnp.float32), *params)
        grads = pullback(seq_cot.astype(jnp.float32))
        new_carry = tuple((total + part_grad for total, part_grad in zip(carry, grads[2:])))
        return (new_carry, (result.astype(jnp.bfloat16), grads[0], grads[1]))
    start_carry = tuple((jnp.zeros(param.shape, jnp.float32) for param in params))
    sums, (output, tokens_grad, condition_grad) = lax.scan(one_sequence, start_carry, (tokens, condition, segment_ids, cotangent))
    g_qkv, g_out, g_up, g_down, g_mod, bias_grad = sums
    block_tiles = jnp.concatenate([g_qkv, g_out, g_up, g_down], axis=0).reshape(NT_W, TR, D)
    block_grad = jnp.zeros((SLOT_ALL_W, TR, D), jnp.float32).at[block_slots].set(block_tiles)
    block_live = jnp.zeros((SLOT_ALL_W,), jnp.float32).at[block_slots].set(1.0)[:, None, None]
    mod_tiles = g_mod.reshape(NT_A, TR, D)
    modulator_grad = jnp.zeros((SLOT_ALL_A, TR, D), jnp.float32).at[modulator_slots].set(mod_tiles)
    mod_live = jnp.zeros((SLOT_ALL_A,), jnp.float32).at[modulator_slots].set(1.0)[:, None, None]
    clip_block = clip_factor(jnp.sum(block_tiles * block_tiles), float(NT_W * TR * D))
    clip_mod = clip_factor(jnp.sum(mod_tiles * mod_tiles), float(NT_A * TR * D))
    clip_bias = clip_factor(jnp.sum(bias_grad * bias_grad), float(NBIAS))
    blk = adam_rule(block_grad, clip_block, block_master, block_first, block_second, block_ema, block_live, learn_rate)
    mdl = adam_rule(modulator_grad, clip_mod, modulator_master, modulator_first, modulator_second, modulator_ema, mod_live, learn_rate)
    bia = adam_rule(bias_grad, clip_bias, biases, bias_first, bias_second, bias_ema, 1.0, bias_rate)
    return (output, tokens_grad, condition_grad, blk[0], blk[1], blk[2], blk[3], blk[4], blk[5], mdl[0], mdl[1], mdl[2], mdl[3], mdl[4], mdl[5], bia[0], bia[1], bia[2], bia[3], bia[4])
```

```python
import jax
import jax.numpy as jnp
from jax import lax
from jax.sharding import PartitionSpec as P

D = 1152
HEADS = 16
HD = 72
FF = 4608
F = 16
PPD = 8
TR = 32
STEP = 5
NT_W = 432
NT_A = 216
LANES = 128


ln_eps = 1e-06
adam_eps = 1e-08
beta_one = 0.5
beta_two = 0.5
learn_rate = 0.01
bias_rate = 0.1
decay_rate = 0.1
ema_rate = 0.9
clip_rms = 0.001
highest = lax.Precision.HIGHEST


def contract_last(left, right):
    return lax.dot_general(
        left, right, (((left.ndim - 1,), (1,)), ((), ())), preferred_element_type=jnp.float32
    )


def contract_first(left, right):
    return lax.dot_general(
        left, right, (((left.ndim - 1,), (0,)), ((), ())), preferred_element_type=jnp.float32
    )


def token_outer(grads, values):
    leading = tuple(range(grads.ndim - 1))
    return lax.dot_general(
        grads, values, ((leading, leading), ((), ())), preferred_element_type=jnp.float32
    )


def norm_rows(values):
    center = values - jnp.mean(values, axis=-1, keepdims=True)
    factor = lax.rsqrt(jnp.mean(center * center, axis=-1, keepdims=True) + ln_eps)
    return (center * factor, factor)


def norm_back(normed, factor, grads):
    return factor * (
        grads
        - jnp.mean(grads, axis=-1, keepdims=True)
        - normed * jnp.mean(grads * normed, axis=-1, keepdims=True)
    )


def swish(values):
    return values * jax.nn.sigmoid(values)


def gelu_tanh(values):
    return jax.nn.gelu(values, approximate=True)


def slope_of(function, values):
    return jax.vjp(function, values)[1](jnp.ones_like(values))[0]


def swap_everywhere(blocks):
    return lax.all_to_all(blocks, ("seq", "batch"), split_axis=0, concat_axis=0, tiled=True)


def sum_everywhere(terms, device_count):
    rows = -(-terms.shape[0] // (device_count * LANES))
    padded = jnp.pad(terms, (0, device_count * rows * LANES - terms.shape[0]))
    mine = jnp.sum(swap_everywhere(padded.reshape(device_count, rows, LANES)), axis=0)
    total = swap_everywhere(jnp.broadcast_to(mine, (device_count, rows, LANES)))
    return total.reshape(-1)[: terms.shape[0]]


def clip_factor(square_sum, count):
    return jnp.minimum(1.0, clip_rms * lax.rsqrt(square_sum / count + 1e-12))


def adam_rule(grads, clip, master, first, second, ema_old, live, rate):
    used = grads * clip
    first_new = beta_one * first + (1.0 - beta_one) * used
    second_new = beta_two * second + (1.0 - beta_two) * used * used
    fix_one = 1.0 - beta_one**STEP
    fix_two = 1.0 - beta_two**STEP
    step_size = rate * (
        first_new / fix_one / (jnp.sqrt(second_new / fix_two) + adam_eps) + decay_rate * master
    )
    master_new = master - step_size
    ema_new = ema_rate * ema_old + (1.0 - ema_rate) * master_new
    return (
        grads * live,
        master_new * live,
        first_new * live,
        second_new * live,
        ema_new * live,
        (master_new * live).astype(jnp.bfloat16),
    )


def on_device(
    tokens,
    condition,
    segment_ids,
    cotangent,
    block_slots,
    modulator_slots,
    block_low,
    block_master,
    block_first,
    block_second,
    block_ema,
    modulator_low,
    modulator_master,
    modulator_first,
    modulator_second,
    modulator_ema,
    biases,
    bias_first,
    bias_second,
    bias_ema,
):
    seq_local = tokens.shape[0]
    frame_rows = tokens.shape[1]
    groups = lax.axis_size("seq")
    batches = lax.axis_size("batch")
    everywhere = ("seq", "batch")
    pair_local = frame_rows // groups
    device_count = lax.axis_size(("seq", "batch"))
    device_place = lax.axis_index(("seq", "batch"))
    block_local = block_low.shape[0]
    modul_local = modulator_low.shape[0]
    tile_of_block = (
        jnp.full((block_local * device_count,), -1, jnp.int32)
        .at[block_slots]
        .set(jnp.arange(NT_W, dtype=jnp.int32))
    )
    tile_of_modul = (
        jnp.full((modul_local * device_count,), -1, jnp.int32)
        .at[modulator_slots]
        .set(jnp.arange(NT_A, dtype=jnp.int32))
    )
    gathered_block = lax.all_gather(block_low, everywhere, axis=0, tiled=True)

    def weight_rows(first, count):
        slots = block_slots[first // TR : (first + count) // TR]
        tiles = gathered_block.at[slots].get(mode="promise_in_bounds")
        return tiles.reshape(count, D)

    w_qkv = weight_rows(0, 3 * D)
    w_out = weight_rows(3 * D, D)
    w_up = weight_rows(4 * D, FF)
    w_down = weight_rows(4 * D + FF, FF)
    b_modul = biases[: 6 * D]
    b_query = biases[6 * D : 7 * D]
    b_value = biases[7 * D : 8 * D]
    b_out = biases[8 * D : 9 * D]
    b_up = biases[9 * D : 9 * D + FF]
    b_down = biases[9 * D + FF :]
    own_rows = modul_local * TR
    cond_float = condition.astype(jnp.float32)
    cond_everyone = lax.all_to_all(
        jnp.tile(condition, (batches, 1)), "batch", split_axis=0, concat_axis=0, tiled=True
    )
    cond_low = swish(cond_everyone.astype(jnp.float32)).astype(jnp.bfloat16)
    modul_rows = modulator_low.reshape(own_rows, D)
    modul_part = contract_last(cond_low, modul_rows).reshape(1, batches, seq_local, own_rows)
    modul_slots = lax.all_to_all(
        jnp.broadcast_to(modul_part, (groups, batches, seq_local, own_rows)).reshape(
            device_count, seq_local, own_rows
        ),
        everywhere,
        split_axis=0,
        concat_axis=0,
        tiled=True,
    )
    modul_slots = jnp.transpose(
        modul_slots.reshape(device_count, seq_local, modul_local, TR), (0, 2, 1, 3)
    ).reshape(device_count * modul_local, seq_local, TR)
    modul = modul_slots.at[modulator_slots].get(mode="promise_in_bounds")
    modul = jnp.transpose(modul, (1, 0, 2)).reshape(seq_local, 6 * D) + b_modul
    shift_one, scale_one, gate_one, shift_two, scale_two, gate_two = [
        piece[:, None, :] for piece in jnp.split(modul, 6, axis=1)
    ]
    x_float = tokens.astype(jnp.float32)
    normed_one, factor_one = norm_rows(x_float)
    act_one = (normed_one * (1.0 + scale_one) + shift_one).astype(jnp.bfloat16)
    patch_one = lax.all_to_all(
        act_one.reshape(seq_local, pair_local, groups, D),
        "seq",
        split_axis=2,
        concat_axis=1,
        tiled=True,
    ).reshape(seq_local, F, PPD, D)
    ids_patch = lax.dynamic_index_in_dim(
        segment_ids.reshape(seq_local, F, PPD, groups),
        lax.axis_index("seq"),
        axis=3,
        keepdims=False,
    )
    ids_order = jnp.transpose(ids_patch, (0, 2, 1))
    same_seg = (ids_order[:, :, :, None] == ids_order[:, :, None, :])[:, :, None]
    qkv_bias = jnp.concatenate([b_query, jnp.zeros((D,), jnp.float32), b_value])
    qkv = contract_last(patch_one, w_qkv) + qkv_bias
    head_shape = (seq_local, F, PPD, HEADS, HD)
    query = qkv[..., :D].astype(jnp.bfloat16).reshape(head_shape)
    keyed = qkv[..., D : 2 * D].astype(jnp.bfloat16).reshape(head_shape)
    valued = qkv[..., 2 * D :].astype(jnp.bfloat16).reshape(head_shape)
    score_scale = HD ** (-0.5)
    scores = (
        jnp.einsum("sfphd,sgphd->sphfg", query, keyed, preferred_element_type=jnp.float32)
        * score_scale
    )
    masked = jnp.where(same_seg, scores, -1e30)
    exps = jnp.exp(masked - jnp.max(masked, axis=-1, keepdims=True))
    probs = exps / jnp.sum(exps, axis=-1, keepdims=True)
    probs_low = probs.astype(jnp.bfloat16)
    attended = jnp.einsum(
        "sphfg,sgphd->sfphd", probs_low, valued, preferred_element_type=jnp.float32
    )
    attended = attended.reshape(seq_local, F, PPD, D).astype(jnp.bfloat16)
    attention_low = (contract_last(attended, w_out) + b_out).astype(jnp.bfloat16)
    frames_attention = lax.all_to_all(
        attention_low.reshape(seq_local, frame_rows, 1, D),
        "seq",
        split_axis=1,
        concat_axis=2,
        tiled=True,
    ).reshape(seq_local, frame_rows, D)
    attention_float = frames_attention.astype(jnp.float32)
    middle = x_float + gate_one * attention_float
    normed_two, factor_two = norm_rows(middle)
    act_two = (normed_two * (1.0 + scale_two) + shift_two).astype(jnp.bfloat16)
    pre_up = contract_last(act_two, w_up) + b_up
    gelu_low = gelu_tanh(pre_up).astype(jnp.bfloat16)
    down = contract_first(gelu_low, w_down) + b_down
    output = (middle + gate_two * down).astype(jnp.bfloat16)
    d_out = cotangent.astype(jnp.float32)
    d_down = (gate_two * d_out).astype(jnp.bfloat16)
    grad_gate_two = jnp.sum(d_out * down, axis=1)
    grad_w_down = token_outer(gelu_low, d_down)
    bias_down = jnp.sum(d_down.astype(jnp.float32), axis=(0, 1))
    d_gelu = contract_last(d_down, w_down)
    d_pre = (d_gelu * slope_of(gelu_tanh, pre_up)).astype(jnp.bfloat16)
    grad_w_up = token_outer(d_pre, act_two)
    bias_up = jnp.sum(d_pre.astype(jnp.float32), axis=(0, 1))
    d_act_two = contract_first(d_pre, w_up)
    grad_shift_two = jnp.sum(d_act_two, axis=1)
    grad_scale_two = jnp.sum(d_act_two * normed_two, axis=1)
    d_middle = d_out + norm_back(normed_two, factor_two, d_act_two * (1.0 + scale_two))
    d_attention = (gate_one * d_middle).astype(jnp.bfloat16)
    grad_gate_one = jnp.sum(d_middle * attention_float, axis=1)
    patch_d_attention = lax.all_to_all(
        d_attention.reshape(seq_local, pair_local, groups, D),
        "seq",
        split_axis=2,
        concat_axis=1,
        tiled=True,
    ).reshape(seq_local, F, PPD, D)
    grad_w_out = token_outer(patch_d_attention, attended)
    bias_out = jnp.sum(patch_d_attention.astype(jnp.float32), axis=(0, 1, 2))
    d_attended = contract_first(patch_d_attention, w_out).astype(jnp.bfloat16).reshape(head_shape)
    d_probs = jnp.einsum(
        "sfphd,sgphd->sphfg", d_attended, valued, preferred_element_type=jnp.float32
    )
    d_value = jnp.einsum(
        "sphfg,sfphd->sgphd", probs_low, d_attended, preferred_element_type=jnp.float32
    )
    d_scores = (probs * (d_probs - jnp.sum(probs * d_probs, axis=-1, keepdims=True))).astype(
        jnp.bfloat16
    )
    d_query = (
        jnp.einsum("sphfg,sgphd->sfphd", d_scores, keyed, preferred_element_type=jnp.float32)
        * score_scale
    )
    d_key = (
        jnp.einsum("sphfg,sfphd->sgphd", d_scores, query, preferred_element_type=jnp.float32)
        * score_scale
    )
    flat_shape = (seq_local, F, PPD, D)
    d_qkv = jnp.concatenate(
        [d_query.reshape(flat_shape), d_key.reshape(flat_shape), d_value.reshape(flat_shape)],
        axis=-1,
    ).astype(jnp.bfloat16)
    grad_w_qkv = token_outer(d_qkv, patch_one)
    d_qkv_float = d_qkv.astype(jnp.float32)
    bias_query = jnp.sum(d_qkv_float[..., :D], axis=(0, 1, 2))
    bias_value = jnp.sum(d_qkv_float[..., 2 * D :], axis=(0, 1, 2))
    d_act_one = contract_first(d_qkv, w_qkv).astype(jnp.bfloat16)
    frames_d_act = (
        lax.all_to_all(
            d_act_one.reshape(seq_local, frame_rows, 1, D),
            "seq",
            split_axis=1,
            concat_axis=2,
            tiled=True,
        )
        .reshape(seq_local, frame_rows, D)
        .astype(jnp.float32)
    )
    grad_shift_one = jnp.sum(frames_d_act, axis=1)
    grad_scale_one = jnp.sum(frames_d_act * normed_one, axis=1)
    tokens_grad = d_middle + norm_back(normed_one, factor_one, frames_d_act * (1.0 + scale_one))
    d_modul = jnp.concatenate(
        [
            grad_shift_one,
            grad_scale_one,
            grad_gate_one,
            grad_shift_two,
            grad_scale_two,
            grad_gate_two,
        ],
        axis=1,
    )
    cond_slope = slope_of(swish, cond_float)
    modul_owned = jnp.where(
        (tile_of_modul >= 0)[:, None, None],
        jnp.transpose(d_modul.reshape(seq_local, NT_A, TR), (1, 0, 2))
        .at[jnp.maximum(tile_of_modul, 0)]
        .get(mode="promise_in_bounds"),
        0.0,
    ).reshape(device_count, modul_local, seq_local, TR)
    d_modul_mine = lax.all_to_all(
        jnp.transpose(modul_owned, (0, 2, 1, 3)).reshape(device_count, seq_local, own_rows),
        everywhere,
        split_axis=0,
        concat_axis=0,
        tiled=True,
    ).reshape(groups, batches * seq_local, own_rows)
    d_modul_mine = jnp.sum(d_modul_mine, axis=0)
    modulator_grad = lax.dot_general(
        d_modul_mine,
        cond_low.astype(jnp.float32),
        (((0,), (0,)), ((), ())),
        precision=highest,
        preferred_element_type=jnp.float32,
    ).reshape(modul_local, TR, D)
    cond_terms = jnp.dot(d_modul_mine, modul_rows.astype(jnp.float32), precision=highest)
    bias_terms = jnp.concatenate(
        [jnp.sum(d_modul, axis=0), bias_query, bias_value, bias_out, bias_up, bias_down]
    )
    bias_count = bias_terms.shape[0]
    small_sums = sum_everywhere(
        jnp.concatenate(
            [
                bias_terms,
                cond_terms.reshape(-1),
                jnp.sum(modulator_grad * modulator_grad)[None],
            ]
        ),
        device_count,
    )
    bias_grad = small_sums[:bias_count]
    cond_sums = small_sums[bias_count : bias_count + cond_terms.size].reshape(cond_terms.shape)
    modul_square = small_sums[bias_count + cond_terms.size]
    condition_grad = cond_slope * lax.dynamic_slice_in_dim(
        cond_sums, lax.axis_index("batch") * seq_local, seq_local
    )
    block_terms = jnp.concatenate(
        [
            grads.astype(jnp.bfloat16).reshape(-1, TR, D)
            for grads in (grad_w_qkv, grad_w_out, grad_w_up, grad_w_down)
        ]
    )
    block_owned = jnp.where(
        (tile_of_block >= 0)[:, None, None],
        block_terms.at[jnp.maximum(tile_of_block, 0)].get(mode="promise_in_bounds"),
        0.0,
    ).astype(jnp.bfloat16)
    block_grad = lax.psum_scatter(
        block_owned, everywhere, scatter_dimension=0, tiled=True
    ).astype(jnp.float32)
    square_terms = jnp.broadcast_to(jnp.sum(block_grad * block_grad), (device_count, 1, LANES))
    block_square = jnp.sum(swap_everywhere(square_terms)[:, 0, 0])
    clip_block = clip_factor(block_square, float(NT_W * TR * D))
    clip_modul = clip_factor(modul_square, float(NT_A * TR * D))
    clip_bias = clip_factor(jnp.sum(bias_grad * bias_grad), float(bias_grad.shape[0]))
    block_mine = lax.dynamic_slice_in_dim(tile_of_block, device_place * block_local, block_local)
    block_live = (block_mine >= 0).astype(jnp.float32)[:, None, None]
    modul_mine = lax.dynamic_slice_in_dim(tile_of_modul, device_place * modul_local, modul_local)
    modul_live = (modul_mine >= 0).astype(jnp.float32)[:, None, None]
    blk = adam_rule(
        block_grad,
        clip_block,
        block_master,
        block_first,
        block_second,
        block_ema,
        block_live,
        learn_rate,
    )
    mdl = adam_rule(
        modulator_grad,
        clip_modul,
        modulator_master,
        modulator_first,
        modulator_second,
        modulator_ema,
        modul_live,
        learn_rate,
    )
    bia = adam_rule(bias_grad, clip_bias, biases, bias_first, bias_second, bias_ema, 1.0, bias_rate)
    return (
        output,
        tokens_grad,
        condition_grad,
        blk[0],
        blk[1],
        blk[2],
        blk[3],
        blk[4],
        blk[5],
        mdl[0],
        mdl[1],
        mdl[2],
        mdl[3],
        mdl[4],
        mdl[5],
        bia[0],
        bia[1],
        bia[2],
        bia[3],
        bia[4],
    )


def solution(mesh):
    placed = (
        P("batch", "seq", None),
        P("batch", None),
        P("batch", None),
        P("batch", "seq", None),
        P(),
        P(),
        P(("seq", "batch"), None, None),
        P(("seq", "batch"), None, None),
        P(("seq", "batch"), None, None),
        P(("seq", "batch"), None, None),
        P(("seq", "batch"), None, None),
        P(("seq", "batch"), None, None),
        P(("seq", "batch"), None, None),
        P(("seq", "batch"), None, None),
        P(("seq", "batch"), None, None),
        P(("seq", "batch"), None, None),
        P(),
        P(),
        P(),
        P(),
    )
    return jax.shard_map(
        on_device,
        mesh=mesh,
        in_specs=placed,
        out_specs=(
            P("batch", "seq", None),
            P("batch", "seq", None),
            P("batch", None),
            P(("seq", "batch"), None, None),
            P(("seq", "batch"), None, None),
            P(("seq", "batch"), None, None),
            P(("seq", "batch"), None, None),
            P(("seq", "batch"), None, None),
            P(("seq", "batch"), None, None),
            P(("seq", "batch"), None, None),
            P(("seq", "batch"), None, None),
            P(("seq", "batch"), None, None),
            P(("seq", "batch"), None, None),
            P(("seq", "batch"), None, None),
            P(("seq", "batch"), None, None),
            P(),
            P(),
            P(),
            P(),
            P(),
        ),
        check_vma=False,
    )
```

```python
import jax
import jax.numpy as jnp
from jax import lax
from jax.sharding import PartitionSpec as P

D = 1152
HEADS = 16
HD = 72
FF = 4608
F = 16
PPD = 8
TR = 32
STEP = 5
NT_W = 432
NT_A = 216
LANES = 128


ln_eps = 1e-06
adam_eps = 1e-08
beta_one = 0.5
beta_two = 0.5
learn_rate = 0.01
bias_rate = 0.1
decay_rate = 0.1
ema_rate = 0.9
clip_rms = 0.001
highest = lax.Precision.HIGHEST


def contract_last(left, right):
    return lax.dot_general(
        left, right, (((left.ndim - 1,), (1,)), ((), ())), preferred_element_type=jnp.float32
    )


def contract_first(left, right):
    return lax.dot_general(
        left, right, (((left.ndim - 1,), (0,)), ((), ())), preferred_element_type=jnp.float32
    )


def token_outer(grads, values):
    leading = tuple(range(grads.ndim - 1))
    return lax.dot_general(
        grads, values, ((leading, leading), ((), ())), preferred_element_type=jnp.float32
    )


def norm_rows(values):
    center = values - jnp.mean(values, axis=-1, keepdims=True)
    factor = lax.rsqrt(jnp.mean(center * center, axis=-1, keepdims=True) + ln_eps)
    return (center * factor, factor)


def norm_back(normed, factor, grads):
    return factor * (
        grads
        - jnp.mean(grads, axis=-1, keepdims=True)
        - normed * jnp.mean(grads * normed, axis=-1, keepdims=True)
    )


def swish(values):
    return values * jax.nn.sigmoid(values)


def gelu_tanh(values):
    return jax.nn.gelu(values, approximate=True)


def slope_of(function, values):
    return jax.vjp(function, values)[1](jnp.ones_like(values))[0]


def swap_everywhere(blocks):
    return lax.all_to_all(blocks, ("seq", "batch"), split_axis=0, concat_axis=0, tiled=True)


def sum_everywhere(terms, device_count):
    rows = -(-terms.shape[0] // (device_count * LANES))
    padded = jnp.pad(terms, (0, device_count * rows * LANES - terms.shape[0]))
    mine = jnp.sum(swap_everywhere(padded.reshape(device_count, rows, LANES)), axis=0)
    total = swap_everywhere(jnp.broadcast_to(mine, (device_count, rows, LANES)))
    return total.reshape(-1)[: terms.shape[0]]


def halve_to_owner(terms, far_first):
    groups, batches = terms.shape[:2]
    seq_bits, batch_bits = groups.bit_length() - 1, batches.bit_length() - 1
    rest = list(range(1, seq_bits))
    order = [0] + (rest[::-1] if far_first else rest)
    steps = [("seq", bit) for bit in order] + [("batch", bit) for bit in range(batch_bits)]
    left = [("seq", bit) for bit in reversed(range(seq_bits))]
    left += [("batch", bit) for bit in reversed(range(batch_bits))]
    terms = terms.reshape((2,) * len(left) + terms.shape[2:])
    for axis, bit in steps:
        dim = left.index((axis, bit))
        left.pop(dim)
        side = (lax.axis_index(axis) >> bit) & 1
        sent = lax.dynamic_index_in_dim(terms, 1 - side, dim, keepdims=False)
        kept = lax.dynamic_index_in_dim(terms, side, dim, keepdims=False)
        pairs = [(place, place ^ (1 << bit)) for place in range(lax.axis_size(axis))]
        arrived = lax.ppermute(sent.astype(jnp.bfloat16), axis, pairs)
        terms = kept.astype(jnp.float32) + arrived.astype(jnp.float32)
    return terms


def clip_factor(square_sum, count):
    return jnp.minimum(1.0, clip_rms * lax.rsqrt(square_sum / count + 1e-12))


def adam_rule(grads, clip, master, first, second, ema_old, live, rate):
    used = grads * clip
    first_new = beta_one * first + (1.0 - beta_one) * used
    second_new = beta_two * second + (1.0 - beta_two) * used * used
    fix_one = 1.0 - beta_one**STEP
    fix_two = 1.0 - beta_two**STEP
    step_size = rate * (
        first_new / fix_one / (jnp.sqrt(second_new / fix_two) + adam_eps) + decay_rate * master
    )
    master_new = master - step_size
    ema_new = ema_rate * ema_old + (1.0 - ema_rate) * master_new
    return (
        grads * live,
        master_new * live,
        first_new * live,
        second_new * live,
        ema_new * live,
        (master_new * live).astype(jnp.bfloat16),
    )


def on_device(
    tokens,
    condition,
    segment_ids,
    cotangent,
    block_slots,
    modulator_slots,
    block_low,
    block_master,
    block_first,
    block_second,
    block_ema,
    modulator_low,
    modulator_master,
    modulator_first,
    modulator_second,
    modulator_ema,
    biases,
    bias_first,
    bias_second,
    bias_ema,
):
    seq_local = tokens.shape[0]
    frame_rows = tokens.shape[1]
    groups = lax.axis_size("seq")
    batches = lax.axis_size("batch")
    everywhere = ("seq", "batch")
    pair_local = frame_rows // groups
    device_count = lax.axis_size(("seq", "batch"))
    device_place = lax.axis_index(("seq", "batch"))
    block_local = block_low.shape[0]
    modul_local = modulator_low.shape[0]
    tile_of_block = (
        jnp.full((block_local * device_count,), -1, jnp.int32)
        .at[block_slots]
        .set(jnp.arange(NT_W, dtype=jnp.int32))
    )
    tile_of_modul = (
        jnp.full((modul_local * device_count,), -1, jnp.int32)
        .at[modulator_slots]
        .set(jnp.arange(NT_A, dtype=jnp.int32))
    )
    gathered_block = lax.all_gather(block_low, everywhere, axis=0, tiled=True)

    def weight_rows(first, count):
        slots = block_slots[first // TR : (first + count) // TR]
        tiles = gathered_block.at[slots].get(mode="promise_in_bounds")
        return tiles.reshape(count, D)

    w_qkv = weight_rows(0, 3 * D)
    w_out = weight_rows(3 * D, D)
    w_up = weight_rows(4 * D, FF)
    w_down = weight_rows(4 * D + FF, FF)
    b_modul = biases[: 6 * D]
    b_query = biases[6 * D : 7 * D]
    b_value = biases[7 * D : 8 * D]
    b_out = biases[8 * D : 9 * D]
    b_up = biases[9 * D : 9 * D + FF]
    b_down = biases[9 * D + FF :]
    own_rows = modul_local * TR
    cond_float = condition.astype(jnp.float32)
    cond_everyone = lax.all_to_all(
        jnp.tile(condition, (batches, 1)), "batch", split_axis=0, concat_axis=0, tiled=True
    )
    cond_low = swish(cond_everyone.astype(jnp.float32)).astype(jnp.bfloat16)
    modul_rows = modulator_low.reshape(own_rows, D)
    modul_part = contract_last(cond_low, modul_rows).reshape(1, batches, seq_local, own_rows)
    modul_slots = lax.all_to_all(
        jnp.broadcast_to(modul_part, (groups, batches, seq_local, own_rows)).reshape(
            device_count, seq_local, own_rows
        ),
        everywhere,
        split_axis=0,
        concat_axis=0,
        tiled=True,
    )
    modul_slots = jnp.transpose(
        modul_slots.reshape(device_count, seq_local, modul_local, TR), (0, 2, 1, 3)
    ).reshape(device_count * modul_local, seq_local, TR)
    modul = modul_slots.at[modulator_slots].get(mode="promise_in_bounds")
    modul = jnp.transpose(modul, (1, 0, 2)).reshape(seq_local, 6 * D) + b_modul
    shift_one, scale_one, gate_one, shift_two, scale_two, gate_two = [
        piece[:, None, :] for piece in jnp.split(modul, 6, axis=1)
    ]
    x_float = tokens.astype(jnp.float32)
    normed_one, factor_one = norm_rows(x_float)
    act_one = (normed_one * (1.0 + scale_one) + shift_one).astype(jnp.bfloat16)
    patch_one = lax.all_to_all(
        act_one.reshape(seq_local, pair_local, groups, D),
        "seq",
        split_axis=2,
        concat_axis=1,
        tiled=True,
    ).reshape(seq_local, F, PPD, D)
    ids_patch = lax.dynamic_index_in_dim(
        segment_ids.reshape(seq_local, F, PPD, groups),
        lax.axis_index("seq"),
        axis=3,
        keepdims=False,
    )
    ids_order = jnp.transpose(ids_patch, (0, 2, 1))
    same_seg = (ids_order[:, :, :, None] == ids_order[:, :, None, :])[:, :, None]
    qkv_bias = jnp.concatenate([b_query, jnp.zeros((D,), jnp.float32), b_value])
    qkv = contract_last(patch_one, w_qkv) + qkv_bias
    head_shape = (seq_local, F, PPD, HEADS, HD)
    query = qkv[..., :D].astype(jnp.bfloat16).reshape(head_shape)
    keyed = qkv[..., D : 2 * D].astype(jnp.bfloat16).reshape(head_shape)
    valued = qkv[..., 2 * D :].astype(jnp.bfloat16).reshape(head_shape)
    score_scale = HD ** (-0.5)
    scores = (
        jnp.einsum("sfphd,sgphd->sphfg", query, keyed, preferred_element_type=jnp.float32)
        * score_scale
    )
    masked = jnp.where(same_seg, scores, -1e30)
    exps = jnp.exp(masked - jnp.max(masked, axis=-1, keepdims=True))
    probs = exps / jnp.sum(exps, axis=-1, keepdims=True)
    probs_low = probs.astype(jnp.bfloat16)
    attended = jnp.einsum(
        "sphfg,sgphd->sfphd", probs_low, valued, preferred_element_type=jnp.float32
    )
    attended = attended.reshape(seq_local, F, PPD, D).astype(jnp.bfloat16)
    attention_low = (contract_last(attended, w_out) + b_out).astype(jnp.bfloat16)
    frames_attention = lax.all_to_all(
        attention_low.reshape(seq_local, frame_rows, 1, D),
        "seq",
        split_axis=1,
        concat_axis=2,
        tiled=True,
    ).reshape(seq_local, frame_rows, D)
    attention_float = frames_attention.astype(jnp.float32)
    middle = x_float + gate_one * attention_float
    normed_two, factor_two = norm_rows(middle)
    act_two = (normed_two * (1.0 + scale_two) + shift_two).astype(jnp.bfloat16)
    pre_up = contract_last(act_two, w_up) + b_up
    gelu_low = gelu_tanh(pre_up).astype(jnp.bfloat16)
    down = contract_first(gelu_low, w_down) + b_down
    output = (middle + gate_two * down).astype(jnp.bfloat16)
    d_out = cotangent.astype(jnp.float32)
    d_down = (gate_two * d_out).astype(jnp.bfloat16)
    grad_gate_two = jnp.sum(d_out * down, axis=1)
    grad_w_down = token_outer(gelu_low, d_down)
    bias_down = jnp.sum(d_down.astype(jnp.float32), axis=(0, 1))
    d_gelu = contract_last(d_down, w_down)
    d_pre = (d_gelu * slope_of(gelu_tanh, pre_up)).astype(jnp.bfloat16)
    grad_w_up = token_outer(d_pre, act_two)
    bias_up = jnp.sum(d_pre.astype(jnp.float32), axis=(0, 1))
    d_act_two = contract_first(d_pre, w_up)
    grad_shift_two = jnp.sum(d_act_two, axis=1)
    grad_scale_two = jnp.sum(d_act_two * normed_two, axis=1)
    d_middle = d_out + norm_back(normed_two, factor_two, d_act_two * (1.0 + scale_two))
    d_attention = (gate_one * d_middle).astype(jnp.bfloat16)
    grad_gate_one = jnp.sum(d_middle * attention_float, axis=1)
    patch_d_attention = lax.all_to_all(
        d_attention.reshape(seq_local, pair_local, groups, D),
        "seq",
        split_axis=2,
        concat_axis=1,
        tiled=True,
    ).reshape(seq_local, F, PPD, D)
    grad_w_out = token_outer(patch_d_attention, attended)
    bias_out = jnp.sum(patch_d_attention.astype(jnp.float32), axis=(0, 1, 2))
    d_attended = contract_first(patch_d_attention, w_out).astype(jnp.bfloat16).reshape(head_shape)
    d_probs = jnp.einsum(
        "sfphd,sgphd->sphfg", d_attended, valued, preferred_element_type=jnp.float32
    )
    d_value = jnp.einsum(
        "sphfg,sfphd->sgphd", probs_low, d_attended, preferred_element_type=jnp.float32
    )
    d_scores = (probs * (d_probs - jnp.sum(probs * d_probs, axis=-1, keepdims=True))).astype(
        jnp.bfloat16
    )
    d_query = (
        jnp.einsum("sphfg,sgphd->sfphd", d_scores, keyed, preferred_element_type=jnp.float32)
        * score_scale
    )
    d_key = (
        jnp.einsum("sphfg,sfphd->sgphd", d_scores, query, preferred_element_type=jnp.float32)
        * score_scale
    )
    flat_shape = (seq_local, F, PPD, D)
    d_qkv = jnp.concatenate(
        [d_query.reshape(flat_shape), d_key.reshape(flat_shape), d_value.reshape(flat_shape)],
        axis=-1,
    ).astype(jnp.bfloat16)
    grad_w_qkv = token_outer(d_qkv, patch_one)
    d_qkv_float = d_qkv.astype(jnp.float32)
    bias_query = jnp.sum(d_qkv_float[..., :D], axis=(0, 1, 2))
    bias_value = jnp.sum(d_qkv_float[..., 2 * D :], axis=(0, 1, 2))
    d_act_one = contract_first(d_qkv, w_qkv).astype(jnp.bfloat16)
    frames_d_act = (
        lax.all_to_all(
            d_act_one.reshape(seq_local, frame_rows, 1, D),
            "seq",
            split_axis=1,
            concat_axis=2,
            tiled=True,
        )
        .reshape(seq_local, frame_rows, D)
        .astype(jnp.float32)
    )
    grad_shift_one = jnp.sum(frames_d_act, axis=1)
    grad_scale_one = jnp.sum(frames_d_act * normed_one, axis=1)
    tokens_grad = d_middle + norm_back(normed_one, factor_one, frames_d_act * (1.0 + scale_one))
    d_modul = jnp.concatenate(
        [
            grad_shift_one,
            grad_scale_one,
            grad_gate_one,
            grad_shift_two,
            grad_scale_two,
            grad_gate_two,
        ],
        axis=1,
    )
    cond_slope = slope_of(swish, cond_float)
    modul_owned = jnp.where(
        (tile_of_modul >= 0)[:, None, None],
        jnp.transpose(d_modul.reshape(seq_local, NT_A, TR), (1, 0, 2))
        .at[jnp.maximum(tile_of_modul, 0)]
        .get(mode="promise_in_bounds"),
        0.0,
    ).reshape(device_count, modul_local, seq_local, TR)
    d_modul_mine = lax.all_to_all(
        jnp.transpose(modul_owned, (0, 2, 1, 3)).reshape(device_count, seq_local, own_rows),
        everywhere,
        split_axis=0,
        concat_axis=0,
        tiled=True,
    ).reshape(groups, batches * seq_local, own_rows)
    d_modul_mine = jnp.sum(d_modul_mine, axis=0)
    modulator_grad = lax.dot_general(
        d_modul_mine,
        cond_low.astype(jnp.float32),
        (((0,), (0,)), ((), ())),
        precision=highest,
        preferred_element_type=jnp.float32,
    ).reshape(modul_local, TR, D)
    cond_terms = jnp.dot(d_modul_mine, modul_rows.astype(jnp.float32), precision=highest)
    bias_terms = jnp.concatenate(
        [jnp.sum(d_modul, axis=0), bias_query, bias_value, bias_out, bias_up, bias_down]
    )
    bias_count = bias_terms.shape[0]
    small_sums = sum_everywhere(
        jnp.concatenate(
            [
                bias_terms,
                cond_terms.reshape(-1),
                jnp.sum(modulator_grad * modulator_grad)[None],
            ]
        ),
        device_count,
    )
    bias_grad = small_sums[:bias_count]
    cond_sums = small_sums[bias_count : bias_count + cond_terms.size].reshape(cond_terms.shape)
    modul_square = small_sums[bias_count + cond_terms.size]
    condition_grad = cond_slope * lax.dynamic_slice_in_dim(
        cond_sums, lax.axis_index("batch") * seq_local, seq_local
    )
    block_terms = jnp.concatenate(
        [
            grads.astype(jnp.bfloat16).reshape(-1, TR, D)
            for grads in (grad_w_qkv, grad_w_out, grad_w_up, grad_w_down)
        ]
    )
    block_mine = lax.dynamic_slice_in_dim(tile_of_block, device_place * block_local, block_local)
    half_terms = block_terms.reshape(NT_W * 2, TR // 2, D)
    owner_tiles = jnp.maximum(tile_of_block, 0).reshape(device_count, block_local)
    chunk = block_local // 2 if block_local % 2 == 0 else block_local
    pieces = []
    for start in range(0, block_local, chunk):
        tiles = owner_tiles[:, start : start + chunk].reshape(-1)
        halves = []
        for half in range(2):
            owned = half_terms.at[tiles * 2 + half].get(mode="promise_in_bounds")
            owned = owned.reshape(groups, batches, chunk, TR // 2, D)
            halves.append(halve_to_owner(owned, half == 1))
        pieces.append(jnp.concatenate(halves, axis=1))
    block_grad = jnp.where(
        (block_mine >= 0)[:, None, None], jnp.concatenate(pieces, axis=0), 0.0
    )
    square_terms = jnp.broadcast_to(jnp.sum(block_grad * block_grad), (device_count, 1, LANES))
    block_square = jnp.sum(swap_everywhere(square_terms)[:, 0, 0])
    clip_block = clip_factor(block_square, float(NT_W * TR * D))
    clip_modul = clip_factor(modul_square, float(NT_A * TR * D))
    clip_bias = clip_factor(jnp.sum(bias_grad * bias_grad), float(bias_grad.shape[0]))
    block_live = (block_mine >= 0).astype(jnp.float32)[:, None, None]
    modul_mine = lax.dynamic_slice_in_dim(tile_of_modul, device_place * modul_local, modul_local)
    modul_live = (modul_mine >= 0).astype(jnp.float32)[:, None, None]
    blk = adam_rule(
        block_grad,
        clip_block,
        block_master,
        block_first,
        block_second,
        block_ema,
        block_live,
        learn_rate,
    )
    mdl = adam_rule(
        modulator_grad,
        clip_modul,
        modulator_master,
        modulator_first,
        modulator_second,
        modulator_ema,
        modul_live,
        learn_rate,
    )
    bia = adam_rule(bias_grad, clip_bias, biases, bias_first, bias_second, bias_ema, 1.0, bias_rate)
    return (
        output,
        tokens_grad,
        condition_grad,
        blk[0],
        blk[1],
        blk[2],
        blk[3],
        blk[4],
        blk[5],
        mdl[0],
        mdl[1],
        mdl[2],
        mdl[3],
        mdl[4],
        mdl[5],
        bia[0],
        bia[1],
        bia[2],
        bia[3],
        bia[4],
    )


def solution(mesh):
    placed = (
        P("batch", "seq", None),
        P("batch", None),
        P("batch", None),
        P("batch", "seq", None),
        P(),
        P(),
        P(("seq", "batch"), None, None),
        P(("seq", "batch"), None, None),
        P(("seq", "batch"), None, None),
        P(("seq", "batch"), None, None),
        P(("seq", "batch"), None, None),
        P(("seq", "batch"), None, None),
        P(("seq", "batch"), None, None),
        P(("seq", "batch"), None, None),
        P(("seq", "batch"), None, None),
        P(("seq", "batch"), None, None),
        P(),
        P(),
        P(),
        P(),
    )
    return jax.shard_map(
        on_device,
        mesh=mesh,
        in_specs=placed,
        out_specs=(
            P("batch", "seq", None),
            P("batch", "seq", None),
            P("batch", None),
            P(("seq", "batch"), None, None),
            P(("seq", "batch"), None, None),
            P(("seq", "batch"), None, None),
            P(("seq", "batch"), None, None),
            P(("seq", "batch"), None, None),
            P(("seq", "batch"), None, None),
            P(("seq", "batch"), None, None),
            P(("seq", "batch"), None, None),
            P(("seq", "batch"), None, None),
            P(("seq", "batch"), None, None),
            P(("seq", "batch"), None, None),
            P(("seq", "batch"), None, None),
            P(),
            P(),
            P(),
            P(),
            P(),
        ),
        check_vma=False,
    )
```
